32 devices in a mesh: dp: 8 (over z, x), mp: 4 (over y, core).
Axes of the slice: x: 2, y: 2, z: 4, core: 2. Of those that a mesh axis runs over, the one named last changes fastest.
Arguments:
- tokens: bfloat16 [16384, 1024], P(('dp', 'mp')), may hold values from -6 to 6
- enc_states: bfloat16 [16, 128, 1024], P('dp'), may hold values from -6 to 6
- lengths: int32 [16], P('dp'), may hold values from 1 to 128, as said below
- cotangent: bfloat16 [16384, 1024], P(('dp', 'mp')), may hold values from -6 to 6
- self_query_key_value_weight: bfloat16 [3, 1024, 1024], P(None, None, 'mp'), may hold values from -0.1875 to 0.1875
- w_self_out: bfloat16 [1024, 1024], P('mp'), may hold values from -0.5 to 0.5
- w_cross_q: bfloat16 [1024, 1024], P(None, 'mp'), may hold values from -0.1875 to 0.1875
- w_cross_kv: bfloat16 [2, 1024, 1024], P(None, None, 'mp'), may hold values from -0.1875 to 0.1875
- w_cross_out: bfloat16 [1024, 1024], P('mp'), may hold values from -0.375 to 0.375
- w_mlp_in: bfloat16 [1024, 4096], P(None, 'mp'), may hold values from -0.1875 to 0.1875
- w_mlp_out: bfloat16 [4096, 1024], P('mp'), may hold values from -0.09375 to 0.09375
- norm_scale: bfloat16 [3, 1024], replicated, may hold values from 0.25 to 1.75
- norm_bias: bfloat16 [3, 1024], replicated, may hold values from -1.5 to 1.5
Outputs:
- block_out: bfloat16 [16384, 1024], P(('dp', 'mp'))
- grad_tokens: float32 [16384, 1024], P(('dp', 'mp'))
- grad_enc: float32 [16, 128, 1024], P('dp', 'mp')
- grad_self_qkv: float32 [3, 1024, 1024], P(None, None, 'mp')
- grad_self_out: float32 [1024, 1024], P('mp')
- grad_cross_q: float32 [1024, 1024], P(None, 'mp')
- grad_cross_kv: float32 [2, 1024, 1024], P(None, None, 'mp')
- grad_cross_out: float32 [1024, 1024], P('mp')
- grad_mlp_in: float32 [1024, 4096], P(None, 'mp')
- grad_mlp_out: float32 [4096, 1024], P('mp')
- grad_norm_scale: float32 [3, 1024], replicated
- grad_norm_bias: float32 [3, 1024], replicated
The draws below stay inside these ranges and needn't reach their ends.
Inputs may be any that keep to these rules, and one draw needn't show every extreme that they name: `lengths`: every caption has at least one position; the first image's caption fills all 128.
All inputs are finite; a program needn't handle non-finite values.
Results may differ from the reference program's by a relative error of at most 0.019.
Values may be sent and summed in bfloat16 or wider, within the bound.
No kernel may reach another device: no remote copies, remote signals or barrier semaphores. Data moves between devices by JAX's collectives and lax.ppermute only.
A program may use at most 192 MiB of HBM per device.

```python
import jax
import jax.numpy as jnp
from jax import lax

D = 1024
H = 16
DH = 64
FF = 4096
DE = 1024
S = 1024
L = 128
IMAGES = 16
TOKENS = 16384


def draw_lengths(key, part):
    first_key, second_key = jax.random.split(jax.random.fold_in(key, 17))
    level = jax.random.randint(first_key, (IMAGES,), 0, 4)
    span = jnp.right_shift(jnp.full((IMAGES,), L, jnp.int32), level)
    fraction = jax.random.randint(second_key, (IMAGES,), 0, 65536)
    drawn = 1 + span * fraction // 65536
    return drawn.astype(jnp.int32).at[0].set(L)


def steps_of(rng, extent, cuts, least, top_value):
    factor_of = 1.0
    for position, blocks in cuts:
        heights = jax.random.uniform(jax.random.fold_in(jax.random.fold_in(rng, 6), position), (blocks,), jnp.float32, least / len(cuts), top_value / len(cuts))
        factor_of = factor_of * jnp.repeat(jnp.exp(heights), extent[position] // blocks).reshape((-1,) + (1,) * (len(extent) - 1 - position))
    return factor_of


def gaussian(own_key, shape, scale, most, shards=(), kind=jnp.bfloat16):
    factor_of = steps_of(own_key, shape, shards, -0.22, 0.18) if shards else 1.0
    entries = jax.random.normal(own_key, shape, jnp.float32) * scale * factor_of
    return jnp.minimum(jnp.maximum(entries, -most), most).astype(kind)


def setup_inputs(seed: int = 0) -> dict:
    splits = jax.random.split(jax.random.key(seed), 14)
    return {
        "tokens": gaussian(splits[0], (TOKENS, D), 1.0, 6.0, ((0, 32),)),
        "enc_states": gaussian(splits[1], (IMAGES, L, DE), 1.0, 6.0, ((0, 8),)),
        "lengths": draw_lengths(jax.random.fold_in(splits[13], 71), 0),
        "cotangent": gaussian(splits[3], (TOKENS, D), 1.0, 6.0, ((0, 32),)),
        "self_query_key_value_weight": gaussian(splits[4], (3, D, H * DH), D ** -0.5, 0.1875, ((2, 4),)),
        "w_self_out": gaussian(splits[5], (H * DH, D), (H * DH // 8) ** -0.5, 0.5, ((0, 4),)),
        "w_cross_q": gaussian(splits[6], (D, H * DH), D ** -0.5, 0.1875, ((1, 4),)),
        "w_cross_kv": gaussian(splits[7], (2, DE, H * DH), DE ** -0.5, 0.1875, ((2, 4),)),
        "w_cross_out": gaussian(splits[8], (H * DH, D), (H * DH // 4) ** -0.5, 0.375, ((0, 4),)),
        "w_mlp_in": gaussian(splits[9], (D, FF), D ** -0.5, 0.1875, ((1, 4),)),
        "w_mlp_out": gaussian(splits[10], (FF, D), FF ** -0.5, 0.09375, ((0, 4),)),
        "norm_scale": jnp.clip(1.0 + 0.15 * jax.random.normal(splits[11], (3, D), jnp.float32), 0.25, 1.75).astype(jnp.bfloat16),
        "norm_bias": gaussian(splits[12], (3, D), 0.3, 1.5),
    }


@jax.custom_vjp
def low(v):
    return lax.optimization_barrier(v.astype(jnp.bfloat16)).astype(jnp.float32)

@jax.custom_vjp
def low_back(v):
    return v

def low_keep(v):
    return (low(v), None)

def low_pass(kept, grad):
    return (grad,)

def backward_retained(v):
    return (v, None)

def back_low(kept, grad):
    return (low(grad),)
low.defvjp(low_keep, low_pass)
low_back.defvjp(backward_retained, back_low)
NORM_EPS = 1e-05
MASK_FILL = -1e+30
HIGHEST = lax.Precision.HIGHEST

def round_both(value):
    return low(low_back(value))

def layer_norm(value, gain, shift):
    center = value - lax.optimization_barrier(jnp.mean(value, -1, keepdims=True))
    spread = lax.optimization_barrier(jnp.mean(center * center, -1, keepdims=True))
    return center * lax.rsqrt(spread + NORM_EPS) * gain + shift

def matmul_hi(left, right):
    return jnp.dot(left, right, precision=HIGHEST)

def image_layer(stream, states, caption_len, wqkv, wso, wcq, wckv, wco, wmi, wmo, gains, shifts):
    seq_len = stream.shape[0]
    score_scale = DH ** (-0.5)
    first_normalized = low(layer_norm(stream, gains[0], shifts[0]))
    proj = round_both(jnp.einsum('sd,tdf->tsf', first_normalized, wqkv, precision=HIGHEST))
    queries = proj[0].reshape(seq_len, H, DH)
    keys_all = proj[1].reshape(seq_len, H, DH)
    values_all = proj[2].reshape(seq_len, H, DH)
    scores = low_back(jnp.einsum('shd,thd->hst', queries, keys_all, precision=HIGHEST) * score_scale)
    positions = jnp.arange(seq_len, dtype=jnp.int32)
    causal = positions[None, :, None] >= positions[None, None, :]
    probs = jax.nn.softmax(jnp.where(causal, scores, MASK_FILL), axis=-1)
    attn = round_both(jnp.einsum('hst,thd->shd', low(probs), values_all, precision=HIGHEST).reshape(seq_len, H * DH))
    mid1 = stream + low_back(matmul_hi(attn, wso))
    normed2 = low(layer_norm(mid1, gains[1], shifts[1]))
    cross_q = round_both(matmul_hi(normed2, wcq)).reshape(seq_len, H, DH)
    cross_kv = round_both(jnp.einsum('ld,tdf->tlf', states, wckv, precision=HIGHEST))
    cross_k = cross_kv[0].reshape(L, H, DH)
    cross_v = cross_kv[1].reshape(L, H, DH)
    cscores = low_back(jnp.einsum('shd,lhd->hsl', cross_q, cross_k, precision=HIGHEST) * score_scale)
    valid = (jnp.arange(L, dtype=jnp.int32) < caption_len)[None, None, :]
    cprobs = jax.nn.softmax(jnp.where(valid, cscores, MASK_FILL), axis=-1)
    cattn = round_both(jnp.einsum('hsl,lhd->shd', low(cprobs), cross_v, precision=HIGHEST).reshape(seq_len, H * DH))
    mid2 = mid1 + low_back(matmul_hi(cattn, wco))
    normed3 = low(layer_norm(mid2, gains[2], shifts[2]))
    hidden = low(jax.nn.gelu(low_back(matmul_hi(normed3, wmi)), approximate=False))
    return mid2 + low_back(matmul_hi(hidden, wmo))

def reference(tokens, enc_states, lengths, cotangent, self_query_key_value_weight, w_self_out, w_cross_q, w_cross_kv, w_cross_out, w_mlp_in, w_mlp_out, norm_scale, norm_bias):
    weights = tuple((w.astype(jnp.float32) for w in (self_query_key_value_weight, w_self_out, w_cross_q, w_cross_kv, w_cross_out, w_mlp_in, w_mlp_out, norm_scale, norm_bias)))
    streams = tokens.astype(jnp.float32).reshape(IMAGES, S, D)
    grads_in = cotangent.astype(jnp.float32).reshape(IMAGES, S, D)
    states_all = enc_states.astype(jnp.float32)

    def step(running, item):
        stream, states, caption_len, grad_out = item

        def forward(stream_in, states_in, *params):
            return image_layer(stream_in, states_in, caption_len, *params)
        result, pullback = jax.vjp(forward, stream, states, *weights)
        grads = pullback(grad_out)
        running = tuple((acc + grad for acc, grad in zip(running, grads[2:])))
        return (running, (result, grads[0], grads[1]))
    start_acc = tuple((jnp.zeros_like(w) for w in weights))
    summed, (results, grad_stream, grad_states) = lax.scan(step, start_acc, (streams, states_all, lengths, grads_in))
    return (results.reshape(TOKENS, D).astype(jnp.bfloat16), grad_stream.reshape(TOKENS, D), grad_states, summed[0], summed[1], summed[2], summed[3], summed[4], summed[5], summed[6], summed[7], summed[8])
```

```python
import jax
import jax.numpy as jnp
from jax import lax
from jax.sharding import PartitionSpec as P

DH = 64
NORM_EPS = 1e-05
MASK_FILL = -1e30
F32 = jnp.float32
BF16 = jnp.bfloat16


def norm_stats(value):
    center = value - jnp.mean(value, -1, keepdims=True)
    rstd = lax.rsqrt(jnp.mean(center * center, -1, keepdims=True) + NORM_EPS)
    return center * rstd, rstd


def layer_norm(value, gain, shift):
    return norm_stats(value)[0] * gain + shift


def norm_back(value, gain, grad):
    hat, rstd = norm_stats(value)
    scaled = grad * gain
    first = jnp.mean(scaled, -1, keepdims=True)
    second = jnp.mean(scaled * hat, -1, keepdims=True)
    return rstd * (scaled - first - hat * second), jnp.sum(grad * hat, 0), jnp.sum(grad, 0)


def mm(left, right):
    return jnp.dot(left, right, preferred_element_type=F32)


def mm_nt(left, right):
    return jnp.einsum("rf,df->rd", left, right, preferred_element_type=F32)


def mm_tn(left, right):
    return jnp.einsum("rd,rf->df", left, right, preferred_element_type=F32)


def exact_gelu(value):
    return jax.nn.gelu(value, approximate=False)


def xor_perm(size, mask):
    return [(i, i ^ mask) for i in range(size)]


def heads_of(value):
    return value.reshape(value.shape[0], -1, DH)


def self_attention(q, k, v, positions):
    s = jnp.einsum("qhd,khd->hqk", heads_of(q), heads_of(k), preferred_element_type=F32) * DH**-0.5
    s = jnp.where(positions[:, None] >= positions[None, :], s, MASK_FILL)
    top = jnp.max(s, -1, keepdims=True)
    e = jnp.exp(s - top)
    total = jnp.sum(e, -1, keepdims=True)
    o = jnp.einsum("hqk,khd->qhd", (e / total).astype(BF16), heads_of(v), preferred_element_type=F32)
    return o.reshape(q.shape).astype(BF16), top + jnp.log(total)


def self_attention_back(q, k, v, lse, da, positions):
    scale = DH**-0.5
    s = jnp.einsum("qhd,khd->hqk", heads_of(q), heads_of(k), preferred_element_type=F32) * scale
    s = jnp.where(positions[:, None] >= positions[None, :], s, MASK_FILL)
    p = jnp.exp(s - lse)
    dp = jnp.einsum("qhd,khd->hqk", heads_of(da), heads_of(v), preferred_element_type=F32)
    ds = (p * (dp - jnp.sum(dp * p, -1, keepdims=True))).astype(BF16)
    dq = jnp.einsum("hqk,khd->qhd", ds, heads_of(k), preferred_element_type=F32) * scale
    dk = jnp.einsum("hqk,qhd->khd", ds, heads_of(q), preferred_element_type=F32) * scale
    dv = jnp.einsum("hqk,qhd->khd", p.astype(BF16), heads_of(da), preferred_element_type=F32)
    return jnp.stack([dq.reshape(q.shape), dk.reshape(q.shape), dv.reshape(q.shape)]).astype(BF16)


def cross_probs(q, k, length):
    s = jnp.einsum("qhd,khd->hqk", heads_of(q), heads_of(k), preferred_element_type=F32) * DH**-0.5
    valid = jnp.arange(k.shape[0]) < length
    return jax.nn.softmax(jnp.where(valid[None, None, :], s, MASK_FILL), axis=-1)


def cross_attention(q, k, v, length):
    p = cross_probs(q, k, length).astype(BF16)
    return (
        jnp.einsum("hqk,khd->qhd", p, heads_of(v), preferred_element_type=F32)
        .reshape(q.shape)
        .astype(BF16)
    )


def cross_attention_back(q, k, v, length, da):
    scale = DH**-0.5
    p = cross_probs(q, k, length)
    dp = jnp.einsum("qhd,khd->hqk", heads_of(da), heads_of(v), preferred_element_type=F32)
    ds = (p * (dp - jnp.sum(dp * p, -1, keepdims=True))).astype(BF16)
    dq = jnp.einsum("hqk,khd->qhd", ds, heads_of(k), preferred_element_type=F32) * scale
    dk = jnp.einsum("hqk,qhd->khd", ds, heads_of(q), preferred_element_type=F32) * scale
    dv = jnp.einsum("hqk,qhd->khd", p.astype(BF16), heads_of(da), preferred_element_type=F32)
    return dq.reshape(q.shape).astype(BF16), dk.reshape(k.shape), dv.reshape(k.shape)


def on_device(
    tokens,
    enc_states,
    lengths,
    cotangent,
    w_qkv,
    w_self_out,
    w_cross_q,
    w_cross_kv,
    w_cross_out,
    w_mlp_in,
    w_mlp_out,
    norm_scale,
    norm_bias,
):
    mp_size = lax.axis_size("mp")
    dp_size = lax.axis_size("dp")
    rows = tokens.shape[0]
    assert mp_size == 4 and enc_states.shape[0] == 2
    assert dp_size & (dp_size - 1) == 0
    dp_bits = dp_size.bit_length() - 1
    me = lax.axis_index("mp")
    group = lax.axis_index("dp")
    core = me % 2
    chip = me // 2
    gains = norm_scale.astype(F32)
    shifts = norm_bias.astype(F32)

    def to_core(value):
        return lax.ppermute(value, "mp", xor_perm(mp_size, 1))

    def to_chip(value):
        return lax.ppermute(value, "mp", xor_perm(mp_size, 2))

    def to_diag(value):
        return lax.ppermute(value, "mp", xor_perm(mp_size, 3))

    def reduce_dp(value, order):
        cur = value
        for bit in order:
            side = (group >> bit) & 1
            half = cur.shape[0] // 2
            keep = lax.dynamic_slice_in_dim(cur, side * half, half, 0)
            send = lax.dynamic_slice_in_dim(cur, (1 - side) * half, half, 0)
            got = lax.ppermute(send, "dp", xor_perm(dp_size, 1 << bit))
            cur = (keep.astype(F32) + got.astype(F32)).astype(BF16)
        for bit in reversed(order):
            side = (group >> bit) & 1
            got = lax.ppermute(cur, "dp", xor_perm(dp_size, 1 << bit))
            cur = jnp.where(
                side == 0, jnp.concatenate([cur, got], 0), jnp.concatenate([got, cur], 0)
            )
        return cur.astype(F32)

    up = tuple(range(dp_bits))
    down = tuple(reversed(up))

    tok_all = jnp.concatenate([tokens, to_core(tokens)], 0)
    cot_all = jnp.concatenate([cotangent, to_core(cotangent)], 0)
    w_qkv_far = to_chip(w_qkv)
    positions = jnp.concatenate(
        [core * rows + jnp.arange(rows), (1 - core) * rows + jnp.arange(rows)]
    )

    normed1 = layer_norm(tok_all.astype(F32), gains[0], shifts[0]).astype(BF16)

    def project(weight):
        return jnp.einsum("uh,bhm->bum", normed1, weight, preferred_element_type=F32).astype(BF16)

    kv_own = jnp.einsum(
        "ild,tdf->itlf", enc_states, w_cross_kv, preferred_element_type=F32
    ).astype(BF16)
    kv_mine = lax.dynamic_index_in_dim(kv_own, chip, 0, keepdims=False)
    kv_other = lax.dynamic_index_in_dim(kv_own, 1 - chip, 0, keepdims=False)
    kv_all = jnp.concatenate(
        [kv_mine, to_chip(kv_other), to_core(kv_mine), to_diag(kv_other)], -1
    )
    length = lax.dynamic_index_in_dim(lengths, chip, 0, keepdims=False)

    def pair_rows(weight):
        pair = jnp.concatenate([weight, to_chip(weight)], 0)
        return jnp.concatenate([pair, to_core(pair)], 0)

    def pair_cols(weight):
        pair = jnp.concatenate([weight, to_chip(weight)], 1)
        return jnp.concatenate([pair, to_core(pair)], 1)

    wso = pair_rows(w_self_out)
    wcq = pair_cols(w_cross_q)
    wco = pair_rows(w_cross_out)
    w_in_far = to_chip(w_mlp_in)
    w_out_far = to_chip(w_mlp_out)

    stream = tokens.astype(F32)
    qkv_own = project(w_qkv)
    attn_own, lse_own = self_attention(qkv_own[0], qkv_own[1], qkv_own[2], positions)
    qkv_far = project(w_qkv_far)
    attn_far, lse_far = self_attention(qkv_far[0], qkv_far[1], qkv_far[2], positions)
    attn_pair = jnp.concatenate([attn_own, attn_far], 1)
    attn = jnp.concatenate([attn_pair[:rows], to_core(attn_pair[rows:])], 1)
    mid1 = stream + mm(attn, wso)
    normed2 = layer_norm(mid1, gains[1], shifts[1]).astype(BF16)
    cross_q = mm(normed2, wcq).astype(BF16)
    cattn = cross_attention(cross_q, kv_all[0], kv_all[1], length)
    mid2 = mid1 + mm(cattn, wco)
    normed3 = layer_norm(mid2, gains[2], shifts[2]).astype(BF16)
    n3_all = jnp.concatenate([normed3, to_core(normed3)], 0)

    def mlp(w_in, w_out):
        pre = mm(n3_all, w_in)
        hidden = exact_gelu(pre).astype(BF16)
        _, gelu_back = jax.vjp(exact_gelu, pre)
        dpre = gelu_back(mm_nt(cot_all, w_out))[0].astype(BF16)
        out = mm(hidden, w_out)
        g_out = mm_tn(hidden, cot_all).astype(BF16)
        g_in = mm_tn(n3_all, dpre).astype(BF16)
        return out, mm_nt(dpre, w_in), g_in, g_out

    out_a, dn3_a, g_in_own, g_out_own = mlp(w_mlp_in, w_mlp_out)
    out_b, dn3_b, g_in_far, g_out_far = mlp(w_in_far, w_out_far)

    def core_scatter(value):
        return value[:rows] + to_core(value[rows:].astype(BF16)).astype(F32)

    def fold_chip(own, far):
        return (own.astype(F32) + to_chip(far).astype(F32)).astype(BF16)

    dn3 = core_scatter(dn3_a + dn3_b)
    block_out = (mid2 + core_scatter(out_a + out_b)).astype(BF16)
    g_mlp_out = reduce_dp(fold_chip(g_out_own, g_out_far), up)
    g_mlp_in = reduce_dp(fold_chip(g_in_own, g_in_far), down)

    grad3 = cotangent.astype(F32)
    dx, gs3, gb3 = norm_back(mid2, gains[2], dn3)
    grad2 = grad3 + dx
    dy2 = grad2.astype(BF16)
    dca = mm_nt(dy2, wco).astype(BF16)
    dqc, dkc, dvc = cross_attention_back(cross_q, kv_all[0], kv_all[1], length, dca)
    width = w_self_out.shape[0]

    def fold_rows(full):
        full = full.astype(BF16)
        pair = (full[: 2 * width].astype(F32) + to_core(full[2 * width :]).astype(F32)).astype(BF16)
        return fold_chip(pair[:width], pair[width:])

    def fold_cols(full):
        full = full.astype(BF16)
        pair = (
            full[:, : 2 * width].astype(F32) + to_core(full[:, 2 * width :]).astype(F32)
        ).astype(BF16)
        return fold_chip(pair[:, :width], pair[:, width:])

    g_cross_out = reduce_dp(fold_rows(mm_tn(cattn, dy2)), up)
    g_cross_q_part = fold_cols(mm_tn(normed2, dqc))

    dkv_part = jnp.stack([dkc, dvc])
    dkv_pair = (
        dkv_part[..., : 2 * width] + to_core(dkv_part[..., 2 * width :])
    ).astype(BF16)
    dkv_mine = dkv_pair[..., :width]
    dkv_other = to_chip(dkv_pair[..., width:])
    enc_mine = lax.dynamic_index_in_dim(enc_states, chip, 0, keepdims=False)
    enc_other = lax.dynamic_index_in_dim(enc_states, 1 - chip, 0, keepdims=False)
    g_cross_kv_part = (
        jnp.einsum("ld,tlf->tdf", enc_mine, dkv_mine, preferred_element_type=F32)
        + jnp.einsum("ld,tlf->tdf", enc_other, dkv_other, preferred_element_type=F32)
    ).astype(BF16)

    def enc_term(dkv):
        return jnp.einsum("tlf,tdf->ld", dkv, w_cross_kv, preferred_element_type=F32)

    dkv_both = jnp.stack([dkv_mine, dkv_other])
    enc_part = jnp.einsum("itlf,tdf->ild", dkv_both, w_cross_kv, preferred_element_type=F32)
    half = enc_part.shape[1] // 2
    keep = lax.dynamic_slice_in_dim(enc_part, chip * half, half, 1)
    send = lax.dynamic_slice_in_dim(enc_part, (1 - chip) * half, half, 1).astype(BF16)
    keep = keep + to_chip(send).astype(F32)[::-1]
    half = half // 2
    enc_sum = lax.dynamic_slice_in_dim(keep, core * half, half, 1)
    send = lax.dynamic_slice_in_dim(keep, (1 - core) * half, half, 1).astype(BF16)
    enc_sum = enc_sum + to_core(send).astype(F32)
    grad_enc = jnp.where(chip == 0, enc_sum, enc_sum[::-1])

    dn2 = mm_nt(dqc, wcq)
    dx, gs2, gb2 = norm_back(mid1, gains[1], dn2)
    grad1 = grad2 + dx
    dy1 = grad1.astype(BF16)
    da = mm_nt(dy1, wso).astype(BF16)
    da_pair = jnp.concatenate([da[:, : 2 * width], to_core(da[:, 2 * width :])], 0)
    g_self_out = reduce_dp(fold_rows(mm_tn(attn, dy1)), down)
    dqkv_far = self_attention_back(
        qkv_far[0], qkv_far[1], qkv_far[2], lse_far, da_pair[:, width:], positions
    )
    dqkv_own = self_attention_back(
        qkv_own[0], qkv_own[1], qkv_own[2], lse_own, da_pair[:, :width], positions
    )

    def qkv_grad(dqkv):
        return jnp.einsum("qc,iqp->icp", normed1, dqkv, preferred_element_type=F32).astype(BF16)

    def qkv_term(dqkv, weight):
        return jnp.einsum("xeh,xkh->ek", dqkv, weight, preferred_element_type=F32)

    g_qkv_part = fold_chip(qkv_grad(dqkv_own), qkv_grad(dqkv_far))
    g_qkv = jnp.stack([reduce_dp(g_qkv_part[i], up if i % 2 else down) for i in range(3)])
    g_cross_q = reduce_dp(g_cross_q_part, up)
    g_cross_kv = jnp.stack([reduce_dp(g_cross_kv_part[i], up if i else down) for i in range(2)])

    dn1 = core_scatter(qkv_term(dqkv_own, w_qkv) + qkv_term(dqkv_far, w_qkv_far))
    dx, gs1, gb1 = norm_back(stream, gains[0], dn1)
    grad_tokens = grad1 + dx
    norms = jnp.stack([gs1, gs2, gs3, gb1, gb2, gb3])
    for bit in range(2):
        norms = norms + lax.ppermute(norms, "mp", xor_perm(mp_size, 1 << bit))
    for bit in up:
        norms = norms + lax.ppermute(norms, "dp", xor_perm(dp_size, 1 << bit))
    return (
        block_out,
        grad_tokens,
        grad_enc,
        g_qkv,
        g_self_out,
        g_cross_q,
        g_cross_kv,
        g_cross_out,
        g_mlp_in,
        g_mlp_out,
        norms[:3],
        norms[3:],
    )


def solution(mesh):
    placed = (
        P(("dp", "mp"), None),
        P("dp", None, None),
        P("dp"),
        P(("dp", "mp"), None),
        P(None, None, "mp"),
        P("mp", None),
        P(None, "mp"),
        P(None, None, "mp"),
        P("mp", None),
        P(None, "mp"),
        P("mp", None),
        P(),
        P(),
    )
    return jax.shard_map(
        on_device,
        mesh=mesh,
        in_specs=placed,
        out_specs=(
            P(("dp", "mp"), None),
            P(("dp", "mp"), None),
            P("dp", "mp", None),
            P(None, None, "mp"),
            P("mp", None),
            P(None, "mp"),
            P(None, None, "mp"),
            P("mp", None),
            P(None, "mp"),
            P("mp", None),
            P(),
            P(),
        ),
        check_vma=False,
    )
```

```python
import functools

import jax
import jax.numpy as jnp
from jax import lax
from jax.experimental import pallas as pl
from jax.experimental.pallas import tpu as pltpu
from jax.sharding import PartitionSpec as P

DH = 64
NORM_EPS = 1e-05
MASK_FILL = -1e30
F32 = jnp.float32
BF16 = jnp.bfloat16
BLOCK = 256


def dot_nn(a, b):
    return jnp.dot(a, b, preferred_element_type=F32)


def dot_nt(a, b):
    return lax.dot_general(a, b, (((1,), (1,)), ((), ())), preferred_element_type=F32)


def dot_tn(a, b):
    return lax.dot_general(a, b, (((0,), (0,)), ((), ())), preferred_element_type=F32)


def whole(shape):
    return pl.BlockSpec(shape, lambda *_: (0,) * len(shape))


def split_heads(value):
    head = lax.broadcasted_iota(jnp.int32, value.shape, 1) // DH
    return [jnp.where(head == h, value, jnp.zeros_like(value)) for h in range(value.shape[1] // DH)]


def causal_tail(s):
    base = s.shape[0] - s.shape[1]
    key = lax.broadcasted_iota(jnp.int32, s.shape, 0) - base
    return jnp.where(key <= lax.broadcasted_iota(jnp.int32, s.shape, 1), s, MASK_FILL)

def absolute(ref, index, shift, blocks):
    parts = []
    for b in range(blocks):
        at = pl.multiple_of(lax.rem(b + shift, blocks) * BLOCK, BLOCK)
        parts.append((b, ref[index, pl.ds(at, BLOCK), :]))
    return parts

def self_fwd_kernel(core_ref, qkv_ref, o_ref, lse_ref, k_ref, vt_ref):
    rows, width = o_ref.shape
    blocks = rows // BLOCK
    heads = width // DH
    i = pl.program_id(0)
    shift = core_ref[0] * (blocks // 2)
    scale = jnp.asarray(DH**-0.5, BF16)

    @pl.when(i == 0)
    def _():
        for b, part in absolute(qkv_ref, 1, shift, blocks):
            k_ref[b * BLOCK : (b + 1) * BLOCK, :] = part * scale
        for b, part in absolute(qkv_ref, 2, shift, blocks):
            vt_ref[:, b * BLOCK : (b + 1) * BLOCK] = part.T
        lse_ref[...] = jnp.zeros_like(lse_ref)

    mine = pl.multiple_of(lax.rem(i + shift, blocks) * BLOCK, BLOCK)

    def attend(n):
        keys = n * BLOCK
        q_heads = split_heads(qkv_ref[0, pl.ds(mine, BLOCK), :])
        k = k_ref[:keys, :]
        scores = [dot_nt(k, q) for q in q_heads]
        outs = []
        for h, s in enumerate(scores):
            s = causal_tail(s)
            top = jnp.max(s, 0, keepdims=True)
            p = jnp.exp(s - top)
            total = jnp.sum(p, 0, keepdims=True)
            lse_ref[h : h + 1, pl.ds(mine, BLOCK)] = top + jnp.log(total)
            out = dot_nn(vt_ref[h * DH : (h + 1) * DH, :keys], p.astype(BF16))
            outs.append(out / total)
        o_ref[pl.ds(mine, BLOCK), :] = jnp.concatenate(outs, 0).T.astype(BF16)

    for n in range(blocks):
        pl.when(i == n)(functools.partial(attend, n + 1))


def self_fwd(core, qkv):
    _, rows, width = qkv.shape
    blocks = rows // BLOCK
    heads = width // DH
    pairs = blocks * (blocks + 1) // 2
    return pl.pallas_call(
        self_fwd_kernel,
        grid_spec=pltpu.PrefetchScalarGridSpec(
            num_scalar_prefetch=1,
            grid=(blocks,),
            in_specs=[whole(qkv.shape)],
            out_specs=[whole((rows, width)), whole((8, rows))],
            scratch_shapes=[
                pltpu.VMEM((rows, width), BF16),
                pltpu.VMEM((width, rows), BF16),
            ],
        ),
        out_shape=[
            jax.ShapeDtypeStruct((rows, width), BF16),
            jax.ShapeDtypeStruct((8, rows), F32),
        ],
        cost_estimate=pl.CostEstimate(
            flops=pairs * heads * 4 * BLOCK * BLOCK * BLOCK,
            bytes_accessed=qkv.size * 2 + rows * width * 2,
            transcendentals=pairs * heads * BLOCK * BLOCK,
        ),
        name="self_fwd",
    )(core, qkv)


def self_bwd_kernel(core_ref, qkv_ref, lse_ref, o_ref, da_ref, out_ref, k_ref, v_ref, kt_ref, dk_ref, dv_ref):
    rows, width = o_ref.shape
    blocks = rows // BLOCK
    heads = width // DH
    i = pl.program_id(0)
    shift = core_ref[0] * (blocks // 2)
    scale = jnp.asarray(DH**-0.5, BF16)

    @pl.when(i == 0)
    def _():
        for b, part in absolute(qkv_ref, 1, shift, blocks):
            part = part * scale
            k_ref[b * BLOCK : (b + 1) * BLOCK, :] = part
            kt_ref[:, b * BLOCK : (b + 1) * BLOCK] = part.T
        for b, part in absolute(qkv_ref, 2, shift, blocks):
            v_ref[b * BLOCK : (b + 1) * BLOCK, :] = part
        dk_ref[...] = jnp.zeros_like(dk_ref)
        dv_ref[...] = jnp.zeros_like(dv_ref)

    mine = pl.multiple_of(lax.rem(i + shift, blocks) * BLOCK, BLOCK)

    def attend(n):
        keys = n * BLOCK
        q_heads = split_heads(qkv_ref[0, pl.ds(mine, BLOCK), :])
        da = da_ref[pl.ds(mine, BLOCK), :]
        da_heads = split_heads(da)
        prod = (da.astype(F32) * o_ref[pl.ds(mine, BLOCK), :].astype(F32)).T
        k = k_ref[:keys, :]
        v = v_ref[:keys, :]
        dqs = []
        dk = dv = None
        for h in range(heads):
            lanes = slice(h * DH, (h + 1) * DH)
            s = causal_tail(dot_nt(k, q_heads[h]))
            dp = dot_nt(v, da_heads[h])
            p = jnp.exp(s - lse_ref[h : h + 1, pl.ds(mine, BLOCK)])
            ds = (p * (dp - jnp.sum(prod[lanes], 0, keepdims=True))).astype(BF16)
            dv_h = dot_nn(p.astype(BF16), da_heads[h])
            dk_h = dot_nn(ds, q_heads[h])
            dv = dv_h if dv is None else dv + dv_h
            dk = dk_h if dk is None else dk + dk_h
            dqs.append(dot_nn(kt_ref[lanes, :keys], ds))
        dv_ref[:keys, :] += dv
        dk_ref[:keys, :] += dk
        out_ref[0, pl.ds(mine, BLOCK), :] = jnp.concatenate(dqs, 0).T.astype(BF16)

    for n in range(blocks):
        pl.when(i == n)(functools.partial(attend, n + 1))

    @pl.when(i == blocks - 1)
    def _():
        for b in range(blocks):
            at = pl.multiple_of(lax.rem(b + shift, blocks) * BLOCK, BLOCK)
            out_ref[1, pl.ds(at, BLOCK), :] = (dk_ref[b * BLOCK : (b + 1) * BLOCK, :] * DH**-0.5).astype(BF16)
            out_ref[2, pl.ds(at, BLOCK), :] = dv_ref[b * BLOCK : (b + 1) * BLOCK, :].astype(BF16)


def self_bwd(core, qkv, lse, o, da):
    _, rows, width = qkv.shape
    blocks = rows // BLOCK
    heads = width // DH
    pairs = blocks * (blocks + 1) // 2
    return pl.pallas_call(
        self_bwd_kernel,
        grid_spec=pltpu.PrefetchScalarGridSpec(
            num_scalar_prefetch=1,
            grid=(blocks,),
            in_specs=[whole(qkv.shape), whole(lse.shape), whole(o.shape), whole(da.shape)],
            out_specs=whole(qkv.shape),
            scratch_shapes=[
                pltpu.VMEM((rows, width), BF16),
                pltpu.VMEM((rows, width), BF16),
                pltpu.VMEM((width, rows), BF16),
                pltpu.VMEM((rows, width), F32),
                pltpu.VMEM((rows, width), F32),
            ],
        ),
        out_shape=jax.ShapeDtypeStruct(qkv.shape, BF16),
        cost_estimate=pl.CostEstimate(
            flops=pairs * heads * 10 * BLOCK * BLOCK * BLOCK,
            bytes_accessed=qkv.size * 4 + rows * width * 4,
            transcendentals=pairs * heads * BLOCK * BLOCK,
        ),
        name="self_bwd",
    )(core, qkv, lse, o, da)


def cross_fwd_kernel(length_ref, q_ref, kv_ref, o_ref):
    heads = q_ref.shape[1] // DH
    q_heads = split_heads(q_ref[...])
    vt = kv_ref[1].T
    k = kv_ref[0] * jnp.asarray(DH**-0.5, BF16)
    scores = [dot_nt(k, q) for q in q_heads]
    live = lax.broadcasted_iota(jnp.int32, scores[0].shape, 0) < length_ref[0]
    outs = []
    for h, s in enumerate(scores):
        s = jnp.where(live, s, MASK_FILL)
        e = jnp.exp(s - jnp.max(s, 0, keepdims=True))
        out = dot_nn(vt[h * DH : (h + 1) * DH], e.astype(BF16))
        outs.append(out / jnp.sum(e, 0, keepdims=True))
    o_ref[...] = jnp.concatenate(outs, 0).T.astype(BF16)

def cross_bwd_kernel(length_ref, q_ref, kv_ref, da_ref, dq_ref, dkv_ref):
    heads = q_ref.shape[1] // DH
    q_heads = split_heads(q_ref[...])
    da_heads = split_heads(da_ref[...])
    k = kv_ref[0] * jnp.asarray(DH**-0.5, BF16)
    v = kv_ref[1]
    kt = k.T
    scores = [dot_nt(k, q) for q in q_heads]
    dps = [dot_nt(v, a) for a in da_heads]
    live = lax.broadcasted_iota(jnp.int32, scores[0].shape, 0) < length_ref[0]
    dqs = []
    dk = None
    dv = None
    for h in range(heads):
        lanes = slice(h * DH, (h + 1) * DH)
        s = jnp.where(live, scores[h], MASK_FILL)
        e = jnp.exp(s - jnp.max(s, 0, keepdims=True))
        p = e / jnp.sum(e, 0, keepdims=True)
        dp = dps[h]
        ds = (p * (dp - jnp.sum(p * dp, 0, keepdims=True))).astype(BF16)
        dv_h = dot_nn(p.astype(BF16), da_heads[h])
        dk_h = dot_nn(ds, q_heads[h])
        dv = dv_h if dv is None else dv + dv_h
        dk = dk_h if dk is None else dk + dk_h
        dqs.append(dot_nn(kt[lanes], ds))
    dq_ref[...] = jnp.concatenate(dqs, 0).T.astype(BF16)

    @pl.when(pl.program_id(0) == 0)
    def _():
        dkv_ref[...] = jnp.zeros_like(dkv_ref)

    dkv_ref[0] += dk * DH**-0.5
    dkv_ref[1] += dv

def cross_fwd(length, q, kv, B=1024):
    rows, width = q.shape
    keys = kv.shape[1]
    return pl.pallas_call(
        cross_fwd_kernel,
        grid_spec=pltpu.PrefetchScalarGridSpec(
            num_scalar_prefetch=1,
            grid=(rows // B,),
            in_specs=[pl.BlockSpec((B, width), lambda i, n: (i, 0)), whole(kv.shape)],
            out_specs=pl.BlockSpec((B, width), lambda i, n: (i, 0)),
        ),
        out_shape=jax.ShapeDtypeStruct(q.shape, BF16),
        cost_estimate=pl.CostEstimate(
            flops=rows * width * keys * 16, bytes_accessed=rows * width * 4, transcendentals=rows * keys * 4
        ),
        name="cross_fwd",
    )(length, q, kv)

def cross_bwd(length, q, kv, da, B=1024):
    rows, width = q.shape
    keys = kv.shape[1]
    tile = pl.BlockSpec((B, width), lambda i, n: (i, 0))
    return pl.pallas_call(
        cross_bwd_kernel,
        grid_spec=pltpu.PrefetchScalarGridSpec(
            num_scalar_prefetch=1,
            grid=(rows // B,),
            in_specs=[tile, whole(kv.shape), tile],
            out_specs=[tile, whole(kv.shape)],
        ),
        out_shape=[jax.ShapeDtypeStruct(q.shape, BF16), jax.ShapeDtypeStruct(kv.shape, F32)],
        cost_estimate=pl.CostEstimate(
            flops=rows * width * keys * 40, bytes_accessed=rows * width * 8, transcendentals=rows * keys * 4
        ),
        name="cross_bwd",
    )(length, q, kv, da)

def gelu_parts(pre):
    cdf = 0.5 * (1.0 + lax.erf(pre * (2.0**-0.5)))
    density = jnp.exp(-0.5 * pre * pre) * 0.3989422804014327
    return pre * cdf, cdf + pre * density


def mlp_kernel(n_ref, dy_ref, wi_ref, wo_ref, hid_ref, dpre_ref):
    for at in range(0, wi_ref.shape[1], BLOCK):
        lanes = slice(at, at + BLOCK)
        pre = dot_nn(n_ref[...], wi_ref[:, lanes])
        back = dot_nt(dy_ref[...], wo_ref[lanes, :])
        value, slope = gelu_parts(pre)
        hid_ref[:, lanes] = value.astype(BF16)
        dpre_ref[:, lanes] = (slope * back).astype(BF16)


def mlp_hidden(n_all, dy_all, w_in, w_out):
    rows, width = n_all.shape
    units = w_in.shape[1]
    tile = pl.BlockSpec((BLOCK, width), lambda r: (r, 0))
    out = pl.BlockSpec((BLOCK, units), lambda r: (r, 0))
    return pl.pallas_call(
        mlp_kernel,
        grid=(rows // BLOCK,),
        in_specs=[tile, tile, whole(w_in.shape), whole(w_out.shape)],
        out_specs=[out, out],
        out_shape=[jax.ShapeDtypeStruct((rows, units), BF16)] * 2,
        cost_estimate=pl.CostEstimate(
            flops=4 * rows * width * units,
            bytes_accessed=rows * width * 8 + units * width * 4,
            transcendentals=2 * rows * units,
        ),
        name="mlp_hidden",
    )(n_all, dy_all, w_in, w_out)


def normalize(value):
    center = value - jnp.mean(value, -1, keepdims=True)
    rstd = lax.rsqrt(jnp.mean(center * center, -1, keepdims=True) + NORM_EPS)
    return center * rstd, rstd


def read_sum(refs, first):
    total = None
    for ref in refs:
        if isinstance(ref, tuple):
            part = jnp.where(first, ref[0][...].astype(F32), ref[1][...].astype(F32))
        else:
            part = ref[...].astype(F32)
        total = part if total is None else total + part
    return total


class Swapped:
    def __init__(self, array):
        self.array = array


def tile_specs(terms, tiles):
    half = tiles // 2
    specs, arrays, shape = [], [], []
    for term in terms:
        if isinstance(term, Swapped):
            width = term.array.shape[1]
            specs.append(pl.BlockSpec((BLOCK, width), lambda r: (lax.rem(r + half, tiles), 0)))
            arrays.append(term.array)
            shape.append(1)
        elif isinstance(term, tuple):
            width = term[0].shape[1]
            specs.append(pl.BlockSpec((BLOCK, width), lambda r: (jnp.minimum(r, half - 1), 0)))
            specs.append(pl.BlockSpec((BLOCK, width), lambda r: (jnp.maximum(r - half, 0), 0)))
            arrays += list(term)
            shape.append(2)
        else:
            specs.append(pl.BlockSpec((BLOCK, term.shape[1]), lambda r: (r, 0)))
            arrays.append(term)
            shape.append(1)
    return specs, arrays, shape


def regroup(refs, shape):
    out, at = [], 0
    for n in shape:
        out.append(tuple(refs[at : at + 2]) if n == 2 else refs[at])
        at += n
    return out


def norm_fwd_kernel(shape, tiles, *refs):
    count = sum(shape)
    terms = regroup(refs[:count], shape)
    gain_ref, shift_ref = refs[count : count + 2]
    outs = refs[count + 2 :]
    total = read_sum(terms, pl.program_id(0) < tiles // 2)
    if len(outs) == 2:
        outs[1][...] = total
    outs[0][...] = (normalize(total)[0] * gain_ref[...] + shift_ref[...]).astype(BF16)


def norm_fwd(terms, gain, shift, rows, keep):
    tiles = rows // BLOCK
    specs, arrays, shape = tile_specs(terms, tiles)
    width = gain.shape[-1]
    tile = pl.BlockSpec((BLOCK, width), lambda r: (r, 0))
    kinds = [BF16, F32] if keep else [BF16]
    return pl.pallas_call(
        functools.partial(norm_fwd_kernel, shape, tiles),
        grid=(tiles,),
        in_specs=specs + [whole((1, width))] * 2,
        out_specs=[tile] * len(kinds),
        out_shape=[jax.ShapeDtypeStruct((rows, width), kind) for kind in kinds],
        cost_estimate=pl.CostEstimate(
            flops=10 * rows * width, bytes_accessed=12 * rows * width, transcendentals=rows
        ),
        name="norm_fwd",
    )(*arrays, gain, shift)


def norm_bwd_kernel(shapes, tiles, *refs):
    shape_v, shape_g, shape_d = shapes
    at = 0
    groups = []
    for shape in shapes:
        groups.append(regroup(refs[at : at + sum(shape)], shape))
        at += sum(shape)
    gain_ref = refs[at]
    outs = refs[at + 1 :]
    first = pl.program_id(0) < tiles // 2
    hat, rstd = normalize(read_sum(groups[0], first))
    grad = read_sum(groups[2], first)
    scaled = grad * gain_ref[...]
    mean = jnp.mean(scaled, -1, keepdims=True)
    cross = jnp.mean(scaled * hat, -1, keepdims=True)
    total = read_sum(groups[1], first) + rstd * (scaled - mean - hat * cross)
    outs[0][...] = total
    if len(outs) == 3:
        outs[1][...] = total.astype(BF16)

    @pl.when(pl.program_id(0) == 0)
    def _():
        outs[-1][...] = jnp.zeros_like(outs[-1])

    outs[-1][0:1, :] += jnp.sum(grad * hat, 0, keepdims=True)
    outs[-1][1:2, :] += jnp.sum(grad, 0, keepdims=True)


def norm_bwd(value, through, grads, gain, rows, low):
    tiles = rows // BLOCK
    specs, arrays, shapes = [], [], []
    for terms in (value, through, grads):
        s, a, shape = tile_specs(terms, tiles)
        specs += s
        arrays += a
        shapes.append(shape)
    width = gain.shape[-1]
    tile = pl.BlockSpec((BLOCK, width), lambda r: (r, 0))
    kinds = [F32, BF16] if low else [F32]
    return pl.pallas_call(
        functools.partial(norm_bwd_kernel, shapes, tiles),
        grid=(tiles,),
        in_specs=specs + [whole((1, width))],
        out_specs=[tile] * len(kinds) + [whole((8, width))],
        out_shape=[jax.ShapeDtypeStruct((rows, width), kind) for kind in kinds]
        + [jax.ShapeDtypeStruct((8, width), F32)],
        cost_estimate=pl.CostEstimate(
            flops=20 * rows * width, bytes_accessed=18 * rows * width, transcendentals=rows
        ),
        name="norm_bwd",
    )(*arrays, gain)


def xor_perm(size, mask):
    return [(i, i ^ mask) for i in range(size)]


class Reduction:
    def __init__(self, values, order, group, size):
        self.group, self.size = group, size
        self.plan = [(bit, True) for bit in order] + [(bit, False) for bit in reversed(order)]
        self.send(values)

    def send(self, values):
        bit, split = self.plan[0]
        side = (self.group >> bit) & 1
        if split:
            half = values[0].shape[0] // 2

            def total(first):
                parts = [lax.dynamic_slice_in_dim(v, first, half, 0).astype(F32) for v in values]
                return sum(parts[1:], parts[0]).astype(BF16)

            out = total((1 - side) * half)
            self.cur = total(side * half)
        else:
            out = self.cur = sum((v.astype(F32) for v in values[1:]), values[0].astype(F32)).astype(
                BF16
            )
        self.got = lax.ppermute(out, "dp", xor_perm(self.size, 1 << bit))

    def tie(self, value):
        if self.got is None:
            return value
        value, self.got = lax.optimization_barrier((value, self.got))
        return value

    def step(self):
        if not self.plan:
            return
        bit, split = self.plan.pop(0)
        if split:
            values = [self.cur, self.got]
        else:
            side = (self.group >> bit) & 1
            values = [
                jnp.where(
                    side == 0,
                    jnp.concatenate([self.cur, self.got], 0),
                    jnp.concatenate([self.got, self.cur], 0),
                )
            ]
        if self.plan:
            self.send(values)
        else:
            self.cur, self.got = values[0], None

    def finish(self):
        while self.plan:
            self.step()
        return self.cur.astype(F32)


def advance(value, *reductions):
    for reduction in reductions:
        value = reduction.tie(value)
    for reduction in reductions:
        reduction.step()
    return value


def on_device(
    tokens,
    enc_states,
    lengths,
    cotangent,
    w_qkv,
    w_self_out,
    w_cross_q,
    w_cross_kv,
    w_cross_out,
    w_mlp_in,
    w_mlp_out,
    norm_scale,
    norm_bias,
):
    mp_size = lax.axis_size("mp")
    dp_size = lax.axis_size("dp")
    half = tokens.shape[0]
    rows = 2 * half
    width = w_self_out.shape[0]
    assert mp_size == 4 and enc_states.shape[0] == 2
    assert dp_size & (dp_size - 1) == 0
    bits = dp_size.bit_length() - 1
    up = tuple(range(bits))
    down = up[1:] + up[:1]
    me = lax.axis_index("mp")
    group = lax.axis_index("dp")
    core = me % 2
    chip = me // 2
    core_arg = core.astype(jnp.int32).reshape(1)
    gains = norm_scale.astype(F32)[:, None, :]
    shifts = norm_bias.astype(F32)[:, None, :]

    def to_core(value):
        return lax.ppermute(value, "mp", xor_perm(mp_size, 1))

    def to_chip(value):
        return lax.ppermute(value, "mp", xor_perm(mp_size, 2))

    def reduction(values, order):
        return Reduction(values, order, group, dp_size)

    tok_pair = (tokens, to_core(tokens))
    w_qkv_far = to_chip(w_qkv)
    kv_both = jnp.einsum(
        "ild,tdf->itlf", enc_states, w_cross_kv, preferred_element_type=F32
    ).astype(BF16)
    kv_own = lax.dynamic_index_in_dim(kv_both, chip, 0, keepdims=False)
    kv_far = to_chip(lax.dynamic_index_in_dim(kv_both, 1 - chip, 0, keepdims=False))
    length = lax.dynamic_slice_in_dim(lengths, chip, 1, 0)
    w_self_out_far = to_chip(w_self_out)
    w_cross_q_far = to_chip(w_cross_q)
    w_cross_out_far = to_chip(w_cross_out)
    cot_pair = (cotangent, to_core(cotangent))
    cot_far = to_chip(cotangent)
    cot_all = jnp.concatenate(cot_pair, 0)
    cot_other = jnp.concatenate([cot_far, to_core(cot_far)], 0)

    (normed1,) = norm_fwd([tok_pair], gains[0], shifts[0], rows, False)

    def project(weight):
        return jnp.einsum("uh,bhm->bum", normed1, weight, preferred_element_type=F32).astype(BF16)

    qkv_own = project(w_qkv)
    attn_own, lse_own = self_fwd(core_arg, qkv_own)
    qkv_far = project(w_qkv_far)
    attn_far, lse_far = self_fwd(core_arg, qkv_far)
    part = (dot_nn(attn_own, w_self_out) + dot_nn(attn_far, w_self_out_far)).astype(BF16)
    normed2, mid1 = norm_fwd([tok_pair, part, Swapped(to_core(part))], gains[1], shifts[1], rows, True)

    cq_own = dot_nn(normed2, w_cross_q).astype(BF16)
    cq_far = dot_nn(normed2, w_cross_q_far).astype(BF16)
    cattn_own = cross_fwd(length, cq_own, kv_own)
    cattn_far = cross_fwd(length, cq_far, kv_far)
    part = (dot_nn(cattn_own, w_cross_out) + dot_nn(cattn_far, w_cross_out_far)).astype(BF16)
    normed3, mid2 = norm_fwd([mid1, part, Swapped(to_core(part))], gains[2], shifts[2], rows, True)

    n3_far = to_chip(normed3[:half])
    n3_other = jnp.concatenate([n3_far, to_core(n3_far)], 0)
    hid_own, dpre_own = mlp_hidden(normed3, cot_all, w_mlp_in, w_mlp_out)
    dn3_part = dot_nt(dpre_own, w_mlp_in).astype(BF16)
    dn3_sib = to_core(dn3_part)
    out_own = dot_nn(hid_own, w_mlp_out).astype(BF16)
    g_out_own = dot_tn(hid_own, cot_all)
    g_in_own = dot_tn(normed3, dpre_own)
    (n3_other, g_out_own, g_in_own, out_own) = lax.optimization_barrier(
        (n3_other, g_out_own, g_in_own, out_own)
    )
    hid_other, dpre_other = mlp_hidden(n3_other, cot_other, w_mlp_in, w_mlp_out)
    dn3_other = dot_nt(dpre_other, w_mlp_in).astype(BF16)
    dn3_send = (dn3_other[:half].astype(F32) + to_core(dn3_other[half:]).astype(F32)).astype(BF16)
    dn3_far = to_chip(dn3_send)
    out_other = dot_nn(hid_other, w_mlp_out).astype(BF16)
    out_send = (out_other[:half].astype(F32) + to_core(out_other[half:]).astype(F32)).astype(BF16)
    red_out = reduction([(g_out_own + dot_tn(hid_other, cot_other)).astype(BF16)], up)
    red_in = reduction([(g_in_own + dot_tn(n3_other, dpre_other)).astype(BF16)], down)
    out_send, dn3_far = lax.optimization_barrier((out_send, dn3_far))
    out_far = to_chip(out_send)

    grad2, dy2, sums3 = norm_bwd(
        [mid2],
        [cot_pair],
        [dn3_part, Swapped(dn3_sib), (dn3_far, to_core(dn3_far))],
        gains[2],
        rows,
        True,
    )

    dca_far = dot_nt(dy2, w_cross_out_far).astype(BF16)
    dca_own = dot_nt(dy2, w_cross_out).astype(BF16)
    dqc_far, dkv_far = cross_bwd(length, cq_far, kv_far, dca_far)
    dqc_own, dkv_own = cross_bwd(length, cq_own, kv_own, dca_own)
    part = (dot_nt(dqc_own, w_cross_q) + dot_nt(dqc_far, w_cross_q_far)).astype(BF16)
    part = advance(part, red_out, red_in)
    part_sib = to_core(part)
    g_far = jnp.concatenate([dot_tn(dy2, cattn_far), dot_tn(normed2, dqc_far)], 0).astype(BF16)
    g_own = jnp.concatenate([dot_tn(dy2, cattn_own), dot_tn(normed2, dqc_own)], 0).astype(BF16)
    dkv_other = to_chip(dkv_far.astype(BF16))
    g_far = to_chip(g_far)
    dkv_mine = dkv_own.astype(BF16)

    grad1, dy1, sums2 = norm_bwd(
        [mid1], [grad2], [part, Swapped(part_sib)], gains[1], rows, True
    )

    da_far = dot_nt(dy1, w_self_out_far).astype(BF16)
    da_far = advance(da_far, red_out, red_in)
    dqkv_far = self_bwd(core_arg, qkv_far, lse_far, attn_far, da_far)
    dqkv_far, g_far = lax.optimization_barrier((dqkv_far, g_far))
    dqkv_far = advance(dqkv_far, red_out, red_in)

    def qkv_grad(dqkv):
        return jnp.einsum("qc,iqp->icp", normed1, dqkv, preferred_element_type=F32).astype(BF16)

    def qkv_term(dqkv, weight):
        return jnp.einsum("xeh,xkh->ek", dqkv, weight, preferred_element_type=F32)

    def bundle(first, rest):
        return jnp.concatenate([first, rest.reshape(-1, width)], 0)

    far_parts = bundle(dot_tn(dy1, attn_far).astype(BF16), qkv_grad(dqkv_far))
    split = far_parts.shape[0] // 2
    far_a = to_chip(far_parts[:split])
    far_b = to_chip(far_parts[split:])

    enc_mine = lax.dynamic_index_in_dim(enc_states, chip, 0, keepdims=False)
    enc_other = lax.dynamic_index_in_dim(enc_states, 1 - chip, 0, keepdims=False)
    g_kv = (
        jnp.einsum("ld,tlf->tdf", enc_mine, dkv_mine, preferred_element_type=F32)
        + jnp.einsum("ld,tlf->tdf", enc_other, dkv_other, preferred_element_type=F32)
    ).astype(BF16)
    red_cross = reduction(
        [bundle((g_own.astype(F32) + g_far.astype(F32)).astype(BF16), g_kv)], up
    )

    da_own = dot_nt(dy1, w_self_out).astype(BF16)
    dqkv_own = self_bwd(core_arg, qkv_own, lse_own, attn_own, da_own)
    dqkv_own = advance(dqkv_own, red_out, red_in, red_cross)
    own_parts = bundle(dot_tn(dy1, attn_own).astype(BF16), qkv_grad(dqkv_own))

    dn1 = (qkv_term(dqkv_own, w_qkv) + qkv_term(dqkv_far, w_qkv_far)).astype(BF16)
    dn1_sib = to_core(dn1[half:])
    own_parts = advance(own_parts, red_out, red_in, red_cross)
    red_a = reduction([own_parts[:split], far_a], down)
    red_b = reduction([own_parts[split:], far_b], up)

    out_sib = to_core(out_own[half:])
    block_out = (
        mid2[:half]
        + out_own[:half].astype(F32)
        + out_sib.astype(F32)
        + out_far.astype(F32)
    ).astype(BF16)
    grad_tokens, sums1 = norm_bwd(
        [tokens], [grad1[:half]], [dn1[:half], dn1_sib], gains[0], half, False
    )

    dkv_both = jnp.stack([dkv_mine, dkv_other])
    enc_part = jnp.einsum("itlf,tdf->ild", dkv_both, w_cross_kv, preferred_element_type=F32)
    span = enc_part.shape[1] // 2
    keep = lax.dynamic_slice_in_dim(enc_part, chip * span, span, 1)
    send = lax.dynamic_slice_in_dim(enc_part, (1 - chip) * span, span, 1).astype(BF16)
    keep = keep + to_chip(send).astype(F32)[::-1]
    span = span // 2
    enc_sum = lax.dynamic_slice_in_dim(keep, core * span, span, 1)
    send = lax.dynamic_slice_in_dim(keep, (1 - core) * span, span, 1).astype(BF16)
    enc_sum = enc_sum + to_core(send).astype(F32)
    grad_enc = jnp.where(chip == 0, enc_sum, enc_sum[::-1])

    norms = jnp.concatenate([sums1[:2], 0.5 * sums2[:2], 0.5 * sums3[:2]], 0)
    for bit in range(2):
        norms = norms + lax.ppermute(norms, "mp", xor_perm(mp_size, 1 << bit))
    for bit in up:
        norms = norms + lax.ppermute(norms, "dp", xor_perm(dp_size, 1 << bit))

    g_mlp_out = red_out.finish()
    g_mlp_in = red_in.finish()
    cross = red_cross.finish()
    first = red_a.finish()
    second = red_b.finish()
    depth = w_cross_q.shape[0]
    g_cross_out = cross[:depth].T
    g_cross_q = cross[depth : 2 * depth]
    g_cross_kv = cross[2 * depth :].reshape(2, depth, width)
    g_self_out = first[:depth].T
    g_qkv = jnp.concatenate([first[depth:], second], 0).reshape(3, depth, width)
    return (
        block_out,
        grad_tokens,
        grad_enc,
        g_qkv,
        g_self_out,
        g_cross_q,
        g_cross_kv,
        g_cross_out,
        g_mlp_in,
        g_mlp_out,
        norms[0::2],
        norms[1::2],
    )


def solution(mesh):
    placed = (
        P(("dp", "mp"), None),
        P("dp", None, None),
        P("dp"),
        P(("dp", "mp"), None),
        P(None, None, "mp"),
        P("mp", None),
        P(None, "mp"),
        P(None, None, "mp"),
        P("mp", None),
        P(None, "mp"),
        P("mp", None),
        P(),
        P(),
    )
    return jax.shard_map(
        on_device,
        mesh=mesh,
        in_specs=placed,
        out_specs=(
            P(("dp", "mp"), None),
            P(("dp", "mp"), None),
            P("dp", "mp", None),
            P(None, None, "mp"),
            P("mp", None),
            P(None, "mp"),
            P(None, None, "mp"),
            P("mp", None),
            P(None, "mp"),
            P("mp", None),
            P(),
            P(),
        ),
        check_vma=False,
    )
```
